256 devices in a mesh: spec: 8 (over x, core), space: 32 (over y, z).
Axes of the slice: x: 4, y: 4, z: 8, core: 2. Of those that a mesh axis runs over, the one named last changes fastest.
Arguments:
- spectra: float32 [768, 256, 128], P(None, ('space', 'spec')), may hold values from -6 to 6
- quad_first: bfloat16 [768, 768], replicated, may hold values from -0.21875 to 0.21875
- quad_second: bfloat16 [768, 768], replicated, may hold values from -0.21875 to 0.21875
- quad_output: bfloat16 [768, 768], replicated, may hold values from -0.21875 to 0.21875
- owner_map: int32 [32], replicated, may hold values from 0 to 2
- land_mask: int32 [256, 128], P('space'), may hold values 0 or 1
- nest_dest: int32 [8192], P('space'), may hold values from 0 to 31, as said below
- nest_src: int32 [8192], P('space'), may hold values from 0 to 1023
- nest_into: int32 [8192], P('space'), may hold values from 0 to 1023
Outputs:
- spectra_out: float32 [768, 256, 128], P(None, ('space', 'spec'))
The draws below stay inside these ranges and needn't reach their ends.
Inputs may be any that keep to these rules, and one draw needn't show every extreme that they name: `nest_dest`: among the 256 entries of each tile no tile is named more than 16 times, and one tile is named exactly 16 times by the entries of every tile.
All inputs are finite; a program needn't handle non-finite values. No bound on the sum of `land_mask` on one device may be relied on, other than what follows from the above.
Results may differ from the reference program's by a relative error of at most 0.0016.
Values sent between devices are 32-bit elements; how exact they have to be, the bound alone decides.
No kernel may reach another device: no remote copies, remote signals or barrier semaphores. Data moves between devices by JAX's collectives and lax.ppermute only.
A program may use at most 64 MiB of HBM per device.

```python
import math
import jax
import jax.numpy as jnp
from jax import lax

BINS = 768
DIRS = 24
LON = 128
SUBSTEPS = 6
GRIDS = 3
CAP = 16
FREQS = 32
TILES = 32
LAT = 256
SEND_DEV = 256
N_SPEC = 8


def draw_nest_dest(key, part):
    busiest = jax.random.randint(jax.random.fold_in(key, 7), (), 0, TILES).astype(jnp.int32)
    repeated = (jnp.arange((TILES - 1) * CAP, dtype=jnp.int32) // CAP).astype(jnp.int32)
    others = repeated + (repeated >= busiest).astype(jnp.int32)

    def sender(sender_index):
        first_key = jax.random.fold_in(jax.random.fold_in(key, 11), sender_index)
        second_key = jax.random.fold_in(jax.random.fold_in(key, 13), sender_index)
        picked = jax.random.permutation(first_key, others)[:SEND_DEV - CAP]
        entries = jnp.concatenate([jnp.full((CAP,), busiest, dtype=jnp.int32), picked.astype(jnp.int32)])
        return jax.random.permutation(second_key, entries)
    return jax.vmap(sender)(jnp.arange(TILES, dtype=jnp.int32)).reshape(TILES * SEND_DEV).astype(jnp.int32)


def set_ends(values, rng, least, high):
    dims = values.shape
    place = [jax.random.randint(jax.random.fold_in(rng, axis), (), 0, dims[axis]) for axis in range(len(dims))]
    values = values.at[tuple(place)].set(least)
    longest = dims.index(max(dims))
    place[longest] = (place[longest] + 1) % dims[longest]
    return values.at[tuple(place)].set(high)


def shard_levels(own_key, shape, pieces, smallest, high):
    gain, own = 1.0, jax.random.fold_in(own_key, 6)
    for position, blocks in pieces:
        steps = jnp.exp(jax.random.uniform(jax.random.fold_in(own, position), (blocks,), jnp.float32, smallest / len(pieces), high / len(pieces)))
        gain = gain * jnp.repeat(steps, shape[position] // blocks).reshape([-1 if axis == position else 1 for axis in range(len(shape))])
    return gain


def noise(own_key, extent, width, limit, split=(), held_as=jnp.bfloat16):
    loudness = shard_levels(own_key, extent, split, -0.22, 0.18) if split else 1.0
    result = jax.random.normal(own_key, extent, jnp.float32) * width * loudness
    return jnp.minimum(jnp.maximum(result, -limit), limit).astype(held_as)


def setup_inputs(seed: int = 0) -> dict:
    seeds = jax.random.split(jax.random.key(seed), 10)
    return {
        "spectra": noise(seeds[0], (BINS, LAT, LON), 1.0, 6.0, ((1, 256),), jnp.float32),
        "quad_first": noise(seeds[1], (BINS, BINS), BINS ** -0.5, 0.21875),
        "quad_second": noise(seeds[2], (BINS, BINS), BINS ** -0.5, 0.21875),
        "quad_output": noise(seeds[3], (BINS, BINS), BINS ** -0.5, 0.21875),
        "owner_map": set_ends(jax.random.randint(seeds[4], (TILES,), 0, GRIDS), jax.random.fold_in(seeds[4], 1), 0, GRIDS - 1).astype(jnp.int32),
        "land_mask": set_ends((jax.random.randint(seeds[5], (LAT, LON), 0, 10) < 7).astype(jnp.int32), jax.random.fold_in(seeds[5], 1), 0, 1),
        "nest_dest": draw_nest_dest(jax.random.fold_in(seeds[9], 71), 0),
        "nest_src": set_ends(jax.random.randint(seeds[7], (TILES * SEND_DEV,), 0, N_SPEC * LON), jax.random.fold_in(seeds[7], 1), 0, (N_SPEC * LON) - 1).astype(jnp.int32),
        "nest_into": set_ends(jax.random.randint(seeds[8], (TILES * SEND_DEV,), 0, N_SPEC * LON), jax.random.fold_in(seeds[8], 1), 0, (N_SPEC * LON) - 1).astype(jnp.int32),
    }


step_weight = 0.25
grid_factors = (1.0, 0.55, 0.3)


def minmod(lower_diff, upper_diff):
    return 0.5 * (jnp.sign(lower_diff) + jnp.sign(upper_diff)) * jnp.minimum(jnp.abs(lower_diff), jnp.abs(upper_diff))


def upwind_sweep(padded, courant, forward, axis_index):
    length = padded.shape[axis_index]
    differences = lax.slice_in_dim(padded, 1, length, axis=axis_index) - lax.slice_in_dim(padded, 0, length - 1, axis=axis_index)
    slopes = minmod(lax.slice_in_dim(differences, 0, length - 2, axis=axis_index), lax.slice_in_dim(differences, 1, length - 1, axis=axis_index))
    centres = lax.slice_in_dim(padded, 1, length - 1, axis=axis_index)
    upper_flux = courant * (centres + 0.5 * (1.0 - courant) * slopes)
    lower_flux = courant * (centres - 0.5 * (1.0 + courant) * slopes)
    face_count = length - 3
    fluxes = jnp.where(forward, lax.slice_in_dim(upper_flux, 0, face_count, axis=axis_index), lax.slice_in_dim(lower_flux, 1, face_count + 1, axis=axis_index))
    interior = lax.slice_in_dim(padded, 2, length - 2, axis=axis_index)
    return interior - (lax.slice_in_dim(fluxes, 1, face_count, axis=axis_index) - lax.slice_in_dim(fluxes, 0, face_count - 1, axis=axis_index))


def bin_speeds(first_bin, bin_count):
    indices = first_bin + jnp.arange(bin_count, dtype=jnp.int32)
    freq_index = (indices // DIRS).astype(jnp.float32)
    direction = ((indices % DIRS).astype(jnp.float32) + 0.5) * (2.0 * math.pi / DIRS)
    speeds = 0.2 + 0.7 * (freq_index + 0.5) / FREQS
    return speeds * jnp.cos(direction), speeds * jnp.sin(direction)


def row_scales(owner_map, first_row, row_count, tile_rows):
    rows_here = first_row + jnp.arange(row_count, dtype=jnp.int32)
    tile_of = jnp.clip(rows_here // tile_rows, 0, owner_map.shape[0] - 1)
    matches = tile_of[:, None] == jnp.arange(owner_map.shape[0], dtype=jnp.int32)[None, :]
    grid_of = jnp.sum(jnp.where(matches, owner_map[None, :], 0), axis=1)
    scales = jnp.where(grid_of == 0, grid_factors[0], jnp.where(grid_of == 1, grid_factors[1], grid_factors[2]))
    return scales.astype(jnp.float32)


def substep(padded, scales, sea_rows, north_speed, east_speed):
    lat_courant = north_speed[:, None, None] * scales[None, 1:-1, None]
    advected = upwind_sweep(padded, lat_courant, (north_speed > 0)[:, None, None], 1)
    lon_padded = jnp.concatenate([advected[:, :, -2:], advected, advected[:, :, :2]], axis=2)
    lon_courant = east_speed[:, None, None] * scales[None, 2:-2, None]
    advected = upwind_sweep(lon_padded, lon_courant, (east_speed > 0)[:, None, None], 2)
    return advected * sea_rows[None]


def source_update(state_field, quad_first, quad_second, quad_output):
    contract = (((0,), (0,)), ((), ()))
    outline = state_field.shape
    matrix = state_field.reshape(outline[0], -1)
    rounded = matrix.astype(jnp.bfloat16)
    linear_one = lax.dot_general(quad_first, rounded, contract, preferred_element_type=jnp.float32)
    linear_two = lax.dot_general(quad_second, rounded, contract, preferred_element_type=jnp.float32)
    product = (linear_one * linear_two).astype(jnp.bfloat16)
    tendency = lax.dot_general(quad_output, product, contract, preferred_element_type=jnp.float32)
    return (matrix + step_weight * tendency).reshape(outline)


def reference(spectra, quad_first, quad_second, quad_output, owner_map, land_mask, nest_dest, nest_src, nest_into):
    sea_mask = land_mask.astype(jnp.float32)
    lat_rows = spectra.shape[1]
    lon_cols = spectra.shape[2]
    state_field = source_update(spectra, quad_first, quad_second, quad_output) * sea_mask[None]
    north_speed, east_speed = bin_speeds(0, BINS)
    scales = row_scales(owner_map, -2, lat_rows + 4, N_SPEC)

    def propagate(blocks):
        block_field, block_north, block_east = blocks
        for counter in range(SUBSTEPS):
            padded = jnp.pad(block_field, ((0, 0), (2, 2), (0, 0)))
            block_field = substep(padded, scales, sea_mask, block_north, block_east)
        return block_field

    grouped = lax.map(propagate, (state_field.reshape(FREQS, DIRS, lat_rows, lon_cols), north_speed.reshape(FREQS, DIRS), east_speed.reshape(FREQS, DIRS)))
    flat_field = grouped.reshape(BINS, lat_rows * lon_cols)
    tile_points = N_SPEC * lon_cols
    senders = jnp.arange(TILES * SEND_DEV, dtype=jnp.int32) // SEND_DEV
    source_cells = senders * tile_points + nest_src
    target_cells = nest_dest * tile_points + nest_into
    totals = jnp.zeros_like(flat_field).at[:, target_cells].add(flat_field[:, source_cells])
    counts = jnp.zeros((lat_rows * lon_cols,), jnp.float32).at[target_cells].add(jnp.ones((TILES * SEND_DEV,), jnp.float32))
    merged = (flat_field + totals) / (1.0 + counts)[None, :]
    finished = source_update(merged.reshape(BINS, lat_rows, lon_cols), quad_first, quad_second, quad_output)
    return finished * sea_mask[None]
```

```python
import math

import jax
import jax.numpy as jnp
from jax import lax
from jax.experimental import pallas as pl
from jax.experimental.pallas import tpu as pltpu
from jax.sharding import PartitionSpec as P

DIRS = 24
SUBSTEPS = 6
FREQS = 32
BINS = 768
LON = 128
LAT = 256
TILES = 32
ROWS = 8
OWN = 3
AUX = 12
STEPS = 32
step_weight = 0.25
grid_factors = (1.0, 0.55, 0.3)


def source_kernel(rank, field, mask, first_hbm, second_hbm, output_hbm, out, first, second, output, sems):
    copies = [
        pltpu.make_async_copy(src, dst, sems.at[n])
        for n, (src, dst) in enumerate(((first_hbm, first), (second_hbm, second), (output_hbm, output)))
    ]
    for copy in copies:
        copy.start()
    state = field[...]
    rounded = state.T.astype(jnp.bfloat16)
    copies[0].wait()
    one = jnp.dot(rounded, first[...], preferred_element_type=jnp.float32)
    copies[1].wait()
    two = jnp.dot(rounded, second[...], preferred_element_type=jnp.float32)
    product = (one * two).astype(jnp.bfloat16)
    copies[2].wait()
    tendency = jnp.dot(product, output[...], preferred_element_type=jnp.float32)
    sea = mask[pl.ds(rank[0], 1), :].astype(jnp.float32)
    out[...] = (state + step_weight * tendency.T) * sea


def source_update(rank, field, mask, quad_first, quad_second, quad_output):
    hbm = pl.BlockSpec(memory_space=pl.ANY)
    vmem = pl.BlockSpec(memory_space=pltpu.VMEM)
    return pl.pallas_call(
        source_kernel,
        out_shape=jax.ShapeDtypeStruct((BINS, LON), jnp.float32),
        in_specs=[pl.BlockSpec(memory_space=pltpu.SMEM), vmem, vmem, hbm, hbm, hbm],
        out_specs=vmem,
        scratch_shapes=[pltpu.VMEM((BINS, BINS), jnp.bfloat16)] * 3 + [pltpu.SemaphoreType.DMA((3,))],
        compiler_params=pltpu.CompilerParams(vmem_limit_bytes=16 * 2**20),
    )(rank, field, mask, quad_first, quad_second, quad_output)


def minmod(lower, upper):
    return jnp.maximum(jnp.minimum(upper, jnp.maximum(lower, 0.0)), jnp.minimum(lower, 0.0))


def transport_kernel(flags, field, aux, coefs, out, state, sea, weighted, columns, summed):
    north_forward = flags[0] > 0
    east_forward = flags[1] > 0
    upwind = jnp.where(east_forward, 1, LON - 1)
    downwind = LON - upwind

    def place(i):
        return jnp.where(north_forward, i, STEPS - 1 - i)

    sublane = lax.broadcasted_iota(jnp.int32, (8, LON), 0)

    def below(value):
        return jnp.where(sublane > 0, pltpu.roll(value, 1, 0), 0.0)

    def above(value):
        return jnp.where(sublane < 7, pltpu.roll(value, 7, 0), 0.0)

    def before(value):
        return jnp.where(north_forward, below(value), above(value))

    def after(value):
        return jnp.where(north_forward, above(value), below(value))

    for i in range(STEPS):
        sea[place(i)] = aux[pl.ds(AUX * (i // 8) + i % 8, 8, stride=AUX * 4), :].astype(jnp.float32)
        for q in range(OWN):
            state[place(i), q] = field[pl.ds(OWN * i + q, 8, stride=OWN * STEPS), :]

    def coef(kind, q, i):
        return coefs[pl.ds(((kind * OWN + q) * 4 + i // 8) * 8, 8), :]

    def flux(kind, q, i, value, slope):
        return coef(kind, q, i) * value + coef(kind + 1, q, i) * slope

    def substep(step, carry):
        here, prev, last, flow = [], [], [], []
        for q in range(OWN):
            start = state[0, q]
            end = state[STEPS - 1, q]
            beyond = after(start)
            slope = minmod(end - state[STEPS - 2, q], beyond - end)
            here.append(start)
            prev.append(start - before(end))
            last.append(beyond)
            flow.append(before(flux(0, q, STEPS - 1, end, slope)))
        for i in range(STEPS):
            for q in range(OWN):
                upper = state[i + 1, q] if i + 1 < STEPS else last[q]
                diff = upper - here[q]
                leaving = flux(0, q, i, here[q], minmod(prev[q], diff))
                value = here[q] - leaving + flow[q]
                here[q], prev[q], flow[q] = upper, diff, leaving
                lower = value - pltpu.roll(value, upwind, 1)
                higher = pltpu.roll(value, downwind, 1) - value
                leaving = flux(2, q, i, value, minmod(lower, higher))
                value = value - leaving + pltpu.roll(leaving, upwind, 1)
                state[i, q] = value * sea[i]
        return carry

    lax.fori_loop(0, SUBSTEPS, substep, 0)

    low_index = lax.broadcasted_iota(jnp.int32, (128, LON), 0)
    high_index = lax.broadcasted_iota(jnp.int32, (256, LON), 0)
    for j in range(4):
        for half in range(2):
            source = aux[pl.ds(AUX * j + 8 + half, 8, stride=AUX * 4), :]
            target = aux[pl.ds(AUX * j + 10 + half, 8, stride=AUX * 4), :]
            source_row = source // LON
            source_col = source % LON
            target_row = target // LON
            target_step = target_row % STEPS
            low = (target_step % 16) * 8 + target_row // STEPS
            high = (target_step // 16) * LON + target % LON
            pieces = []
            for q in range(OWN):
                taken = jnp.zeros((8, LON), jnp.float32)
                for r in range(ROWS):
                    row = state[place(8 * j + r), q]
                    taken = jnp.where(source_row == r, jnp.take_along_axis(row, source_col, axis=1), taken)
                coarse = taken.astype(jnp.bfloat16)
                wide = coarse.astype(jnp.float32)
                pieces += [wide, taken - wide]
            pieces.append(jnp.ones((8, LON), jnp.float32))
            for g in range(8):
                at = ((j * 2 + half) * 8 + g) * LON
                hit = low_index == low[g : g + 1, :]
                for n, piece in enumerate(pieces):
                    chosen = jnp.where(hit, piece[g : g + 1, :], 0.0)
                    weighted[n * 128 : n * 128 + 128, at : at + LON] = chosen.astype(jnp.bfloat16)
                hit = high_index == high[g : g + 1, :]
                columns[:, at : at + LON] = jnp.where(hit, 1.0, 0.0).astype(jnp.bfloat16)
    summed[...] = lax.dot_general(
        weighted[...], columns[...], (((1,), (1,)), ((), ())), preferred_element_type=jnp.float32
    )
    for i in range(STEPS):
        top = (i % 16) * 8
        left = (i // 16) * LON

        def block(n):
            return summed[n * 128 + top : n * 128 + top + 8, left : left + LON]

        share = 1.0 / (1.0 + block(2 * OWN))
        for q in range(OWN):
            merged = (state[place(i), q] + (block(2 * q) + block(2 * q + 1))) * share
            out[pl.ds(OWN * i + q, 8, stride=OWN * STEPS), :] = merged


def transport(flags, field, aux, coefs):
    vmem = pl.BlockSpec(memory_space=pltpu.VMEM)
    entries = TILES * LAT
    return pl.pallas_call(
        transport_kernel,
        out_shape=jax.ShapeDtypeStruct((BINS, LON), jnp.float32),
        in_specs=[pl.BlockSpec(memory_space=pltpu.SMEM), vmem, vmem, vmem],
        out_specs=vmem,
        scratch_shapes=[
            pltpu.VMEM((STEPS, OWN, 8, LON), jnp.float32),
            pltpu.VMEM((STEPS, 8, LON), jnp.float32),
            pltpu.VMEM(((2 * OWN + 1) * 128, entries), jnp.bfloat16),
            pltpu.VMEM((256, entries), jnp.bfloat16),
            pltpu.VMEM(((2 * OWN + 1) * 128, 256), jnp.float32),
        ],
        compiler_params=pltpu.CompilerParams(vmem_limit_bytes=40 * 2**20),
    )(flags, field, aux, coefs)


def bin_speeds(first_bin, bin_count):
    indices = first_bin + jnp.arange(bin_count, dtype=jnp.int32)
    freq_index = (indices // DIRS).astype(jnp.float32)
    direction = ((indices % DIRS).astype(jnp.float32) + 0.5) * (2.0 * math.pi / DIRS)
    speeds = 0.2 + 0.7 * (freq_index + 0.5) / FREQS
    return (speeds * jnp.cos(direction), speeds * jnp.sin(direction))


def shards(
    spectra,
    quad_first,
    quad_second,
    quad_output,
    owner_map,
    land_mask,
    nest_dest,
    nest_src,
    nest_into,
):
    everyone = ("space", "spec")
    spec_rank = lax.axis_index("spec")
    device = lax.axis_index("space") * lax.axis_size("spec") + spec_rank
    rank = spec_rank.reshape(1)
    target = nest_dest * (ROWS * LON) + nest_into
    lists = jnp.concatenate([land_mask.reshape(-1), nest_src, target])
    lists = jnp.broadcast_to(lists, (TILES, 1, AUX * LON))
    aux = lax.all_to_all(lists, "space", split_axis=0, concat_axis=0, tiled=True).reshape(TILES * AUX, LON)
    north, east = bin_speeds(device * OWN, OWN)
    flags = jnp.stack([north[0] > 0, east[0] > 0]).astype(jnp.int32)
    scales = jnp.where(
        owner_map == 0, grid_factors[0], jnp.where(owner_map == 1, grid_factors[1], grid_factors[2])
    ).astype(jnp.float32)
    scales = scales.reshape(8, 4).T
    scales = jnp.where(north[0] > 0, scales, scales[::-1])
    lat = jnp.abs(north)[:, None, None] * scales[None]
    lon = jnp.abs(east)[:, None, None] * scales[None]
    coefs = jnp.stack([lat, 0.5 * lat * (1.0 - lat), lon, 0.5 * lon * (1.0 - lon)])
    coefs = jnp.broadcast_to(coefs[..., None], coefs.shape + (LON,)).reshape(-1, LON)
    sourced = source_update(rank, spectra.reshape(BINS, LON), land_mask, quad_first, quad_second, quad_output)
    banded = lax.all_to_all(
        sourced.reshape(LAT, 1, OWN * LON), everyone, split_axis=0, concat_axis=0, tiled=True
    ).reshape(BINS, LON)
    merged = transport(flags, banded, aux, coefs)
    rows = lax.all_to_all(
        merged.reshape(LAT, 1, OWN * LON), everyone, split_axis=0, concat_axis=0, tiled=True
    ).reshape(BINS, LON)
    finished = source_update(rank, rows, land_mask, quad_first, quad_second, quad_output)
    return finished.reshape(BINS, 1, LON)


def solution(mesh):
    return jax.shard_map(
        shards,
        mesh=mesh,
        in_specs=(
            P(None, ("space", "spec"), None),
            P(),
            P(),
            P(),
            P(),
            P("space", None),
            P("space"),
            P("space"),
            P("space"),
        ),
        out_specs=P(None, ("space", "spec"), None),
        check_vma=False,
    )
```

```python
import math

import jax
import jax.numpy as jnp
from jax import lax
from jax.experimental import pallas as pl
from jax.experimental.pallas import tpu as pltpu
from jax.sharding import PartitionSpec as P

DIRS = 24
SUBSTEPS = 6
FREQS = 32
BINS = 768
LON = 128
LAT = 256
ROWS = 8
ENTRIES = 8192
OWN = 3
SENT = 5
STEPS = 32
PIECES = 2 * OWN + 1
step_weight = 0.25
grid_factors = (1.0, 0.55, 0.3)


def tendency_of(state, first, second, output, wait):
    rounded = state.T.astype(jnp.bfloat16)
    wait(0)
    one = jnp.dot(rounded, first[...], preferred_element_type=jnp.float32)
    wait(1)
    two = jnp.dot(rounded, second[...], preferred_element_type=jnp.float32)
    product = (one * two).astype(jnp.bfloat16)
    wait(2)
    return jnp.dot(product, output[...], preferred_element_type=jnp.float32).T


def send_kernel(
    rank,
    field_hbm,
    mask_hbm,
    dest_hbm,
    src_hbm,
    into_hbm,
    first_hbm,
    second_hbm,
    output_hbm,
    out,
    field,
    mask,
    dest,
    src,
    into,
    first,
    second,
    output,
    sourced,
    sems,
):
    pairs = (
        (first_hbm, first),
        (second_hbm, second),
        (output_hbm, output),
        (field_hbm, field),
        (mask_hbm, mask),
        (dest_hbm, dest),
        (src_hbm, src),
        (into_hbm, into),
    )
    copies = [pltpu.make_async_copy(a, b, sems.at[n]) for n, (a, b) in enumerate(pairs)]
    for n in (3, 4, 5, 6, 7, 0, 1, 2):
        copies[n].start()
    for n in (3, 4, 5, 6, 7):
        copies[n].wait()
    state = field[...]
    sea = mask[pl.ds(rank[0], 1), :].astype(jnp.float32)
    part = rank[0] % 4
    wanted = lax.broadcasted_iota(jnp.int32, (2, LON), 0) == rank[0] // 4
    lane = lax.broadcasted_iota(jnp.int32, (8, LON), 1)

    def entries(value, shift):
        row = jnp.sum(jnp.where(wanted, value, 0), axis=0, keepdims=True).astype(jnp.float32)
        return pltpu.roll(jnp.broadcast_to(row, (8, LON)), shift, 1)

    lists = jnp.where(lane < 32, entries(src[...], (LON - 32 * part) % LON), 0.0)
    target = entries(dest[...] * (ROWS * LON) + into[...], (LON + 32 - 32 * part) % LON)
    lists = jnp.where((lane >= 32) & (lane < 64), target, lists)
    wide = jnp.broadcast_to(sea, (8, LON))
    for n in range(LAT // 8):
        out[pl.ds(SENT * 8 * n + OWN, 8, stride=SENT), :] = wide
        out[pl.ds(SENT * 8 * n + OWN + 1, 8, stride=SENT), :] = lists
    tendency = tendency_of(state, first, second, output, lambda n: copies[n].wait())
    sourced[...] = (state + step_weight * tendency) * sea
    for n in range(LAT // 8):
        for q in range(OWN):
            out[pl.ds(SENT * 8 * n + q, 8, stride=SENT), :] = sourced[pl.ds(OWN * 8 * n + q, 8, stride=OWN), :]


def source_and_pack(rank, field, mask, dest, src, into, first, second, output):
    hbm = pl.BlockSpec(memory_space=pltpu.HBM)
    square = pltpu.VMEM((BINS, BINS), jnp.bfloat16)
    pair = pltpu.VMEM((2, LON), jnp.int32)
    return pl.pallas_call(
        send_kernel,
        out_shape=jax.ShapeDtypeStruct((LAT * SENT, LON), jnp.float32),
        in_specs=[pl.BlockSpec(memory_space=pltpu.SMEM)] + [hbm] * 8,
        out_specs=pl.BlockSpec(memory_space=pltpu.VMEM),
        scratch_shapes=[
            pltpu.VMEM((BINS, LON), jnp.float32),
            pltpu.VMEM((ROWS, LON), jnp.int32),
            pair,
            pair,
            pair,
            square,
            square,
            square,
            pltpu.VMEM((BINS, LON), jnp.float32),
            pltpu.SemaphoreType.DMA((8,)),
        ],
        compiler_params=pltpu.CompilerParams(vmem_limit_bytes=62 * 2**20),
    )(rank, field, mask, dest, src, into, first, second, output)


def finish_kernel(rank, field, mask, first, second, output, out):
    state = field[...]
    sea = mask[pl.ds(rank[0], 1), :].astype(jnp.float32)
    out[...] = (state + step_weight * tendency_of(state, first, second, output, lambda n: None)) * sea


def source_update(rank, field, mask, first, second, output):
    vmem = pl.BlockSpec(memory_space=pltpu.VMEM)
    return pl.pallas_call(
        finish_kernel,
        out_shape=jax.ShapeDtypeStruct((BINS, LON), jnp.float32),
        in_specs=[pl.BlockSpec(memory_space=pltpu.SMEM)] + [vmem] * 5,
        out_specs=vmem,
        compiler_params=pltpu.CompilerParams(vmem_limit_bytes=16 * 2**20),
    )(rank, field, mask, first, second, output)


def minmod(lower, upper):
    return jnp.maximum(jnp.minimum(upper, jnp.maximum(lower, 0.0)), jnp.minimum(lower, 0.0))


def transport_kernel(device, owners, field, out, state, sea, coefs, weighted, columns, summed):
    first_bin = device[0] * OWN
    first_dir = first_bin % DIRS
    north_forward = (first_dir < DIRS // 4) | (first_dir >= DIRS - DIRS // 4)
    east_forward = first_dir < DIRS // 2
    upwind = jnp.where(east_forward, 1, LON - 1)
    downwind = LON - upwind

    def place(i):
        return jnp.where(north_forward, i, STEPS - 1 - i)

    def received(i, n):
        return field[pl.ds(SENT * i + n, 8, stride=SENT * STEPS), :]

    sublane = lax.broadcasted_iota(jnp.int32, (8, LON), 0)
    lane = lax.broadcasted_iota(jnp.int32, (8, LON), 1)

    def below(value):
        return jnp.where(sublane > 0, pltpu.roll(value, 1, 0), 0.0)

    def above(value):
        return jnp.where(sublane < 7, pltpu.roll(value, 7, 0), 0.0)

    def before(value):
        return jnp.where(north_forward, below(value), above(value))

    def after(value):
        return jnp.where(north_forward, above(value), below(value))

    for j in range(4):
        scale = jnp.zeros((8, LON), jnp.float32)
        for g in range(8):
            owner = owners[4 * g + jnp.where(north_forward, j, 3 - j)]
            factor = jnp.where(owner == 0, grid_factors[0], jnp.where(owner == 1, grid_factors[1], grid_factors[2]))
            scale = jnp.where(sublane == g, factor, scale)
        for q in range(OWN):
            splat = jnp.zeros((8, LON), jnp.int32) + (first_bin + q)
            direction = ((splat % DIRS).astype(jnp.float32) + 0.5) * (2.0 * math.pi / DIRS)
            speed = 0.2 + 0.7 * ((splat // DIRS).astype(jnp.float32) + 0.5) / FREQS
            north = jnp.abs(speed * jnp.cos(direction)) * scale
            east = jnp.abs(speed * jnp.sin(direction)) * scale
            for kind, value in enumerate(
                (north, 0.5 * north * (1.0 - north), east, 0.5 * east * (1.0 - east))
            ):
                coefs[(kind * OWN + q) * 4 + j] = value
    for i in range(STEPS):
        sea[place(i)] = received(i, OWN)
        for q in range(OWN):
            state[place(i), q] = received(i, q)

    def coef(kind, q, i):
        return coefs[(kind * OWN + q) * 4 + i // 8]

    def flux(kind, q, i, value, slope):
        return coef(kind, q, i) * value + coef(kind + 1, q, i) * slope

    for step in range(SUBSTEPS):
        here, prev, last, flow = [], [], [], []
        for q in range(OWN):
            start = state[0, q]
            end = state[STEPS - 1, q]
            beyond = after(start)
            slope = minmod(end - state[STEPS - 2, q], beyond - end)
            here.append(start)
            prev.append(start - before(end))
            last.append(beyond)
            flow.append(before(flux(0, q, STEPS - 1, end, slope)))
        for i in range(STEPS):
            for q in range(OWN):
                upper = state[i + 1, q] if i + 1 < STEPS else last[q]
                diff = upper - here[q]
                leaving = flux(0, q, i, here[q], minmod(prev[q], diff))
                value = here[q] - leaving + flow[q]
                here[q], prev[q], flow[q] = upper, diff, leaving
                lower = value - pltpu.roll(value, upwind, 1)
                higher = pltpu.roll(value, downwind, 1) - value
                leaving = flux(2, q, i, value, minmod(lower, higher))
                value = value - leaving + pltpu.roll(leaving, upwind, 1)
                state[i, q] = value * sea[i]

    def spread(row, times):
        pair = jnp.broadcast_to(row, (16, LON)).astype(jnp.bfloat16)
        return jnp.broadcast_to(pair[None], (times, 16, LON)).reshape(times * 16, LON)

    low_index = lax.broadcasted_iota(jnp.int32, (128, LON), 0).astype(jnp.float32).astype(jnp.bfloat16)
    high_index = lax.broadcasted_iota(jnp.int32, (256, LON), 0).astype(jnp.float32).astype(jnp.bfloat16)
    zero = jnp.zeros((), jnp.bfloat16)
    one = jnp.ones((), jnp.bfloat16)
    for j in range(4):
        for half in range(2):
            source = target = jnp.zeros((8, LON), jnp.float32)
            for k in range(4):
                lists = received(8 * j + 4 * half + k, OWN + 1)
                inside = (lane >= 32 * k) & (lane < 32 * k + 32)
                source = jnp.where(inside, pltpu.roll(lists, 32 * k, 1) if k else lists, source)
                target = jnp.where(inside, pltpu.roll(lists, (32 * k + 96) % LON, 1) if k != 1 else lists, target)
            source = source.astype(jnp.int32)
            target = target.astype(jnp.int32)
            source_row = source // LON
            source_col = source % LON
            target_row = target // LON
            target_step = target_row % STEPS
            low = ((target_step % 16) * 8 + target_row // STEPS).astype(jnp.float32)
            high = ((target_step // 16) * LON + target % LON).astype(jnp.float32)
            pieces = []
            for q in range(OWN):
                taken = jnp.zeros((8, LON), jnp.float32)
                for r in range(ROWS):
                    row = state[place(8 * j + r), q]
                    taken = jnp.where(source_row == r, jnp.take_along_axis(row, source_col, axis=1), taken)
                coarse = taken.astype(jnp.bfloat16).astype(jnp.float32)
                pieces += [coarse, taken - coarse]
            pieces.append(jnp.ones((8, LON), jnp.float32))
            for g in range(8):
                at = ((j * 2 + half) * 8 + g) * LON
                hit = low_index == spread(low[g : g + 1, :], 8)
                for n, piece in enumerate(pieces):
                    weighted[n * 128 : n * 128 + 128, at : at + LON] = jnp.where(hit, spread(piece[g : g + 1, :], 8), zero)
                hit = high_index == spread(high[g : g + 1, :], 16)
                columns[:, at : at + LON] = jnp.where(hit, one, zero)
    summed[...] = lax.dot_general(
        weighted[...], columns[...], (((1,), (1,)), ((), ())), preferred_element_type=jnp.float32
    )
    for i in range(STEPS):
        top = (i % 16) * 8
        left = (i // 16) * LON

        def block(n):
            return summed[n * 128 + top : n * 128 + top + 8, left : left + LON]

        share = 1.0 / (1.0 + block(2 * OWN))
        for q in range(OWN):
            merged = (state[place(i), q] + (block(2 * q) + block(2 * q + 1))) * share
            out[pl.ds(OWN * i + q, 8, stride=OWN * STEPS), :] = merged


def transport(device, owners, field):
    vmem = pl.BlockSpec(memory_space=pltpu.VMEM)
    smem = pl.BlockSpec(memory_space=pltpu.SMEM)
    return pl.pallas_call(
        transport_kernel,
        out_shape=jax.ShapeDtypeStruct((BINS, LON), jnp.float32),
        in_specs=[smem, smem, vmem],
        out_specs=vmem,
        scratch_shapes=[
            pltpu.VMEM((STEPS, OWN, 8, LON), jnp.float32),
            pltpu.VMEM((STEPS, 8, LON), jnp.float32),
            pltpu.VMEM((4 * OWN * 4, 8, LON), jnp.float32),
            pltpu.VMEM((PIECES * 128, ENTRIES), jnp.bfloat16),
            pltpu.VMEM((256, ENTRIES), jnp.bfloat16),
            pltpu.VMEM((PIECES * 128, 256), jnp.float32),
        ],
        compiler_params=pltpu.CompilerParams(vmem_limit_bytes=32 * 2**20),
    )(device, owners, field)


def shards(
    spectra,
    quad_first,
    quad_second,
    quad_output,
    owner_map,
    land_mask,
    nest_dest,
    nest_src,
    nest_into,
):
    everyone = ("space", "spec")
    spec_rank = lax.axis_index("spec")
    device = lax.axis_index("space") * lax.axis_size("spec") + spec_rank
    rank = spec_rank.reshape(1)
    sent = source_and_pack(
        rank,
        spectra.reshape(BINS, LON),
        land_mask,
        nest_dest.reshape(2, LON),
        nest_src.reshape(2, LON),
        nest_into.reshape(2, LON),
        quad_first,
        quad_second,
        quad_output,
    )
    banded = lax.all_to_all(
        sent.reshape(LAT, 1, SENT * LON), everyone, split_axis=0, concat_axis=0, tiled=True
    ).reshape(LAT * SENT, LON)
    merged = transport(device.reshape(1), owner_map, banded)
    rows = lax.all_to_all(
        merged.reshape(LAT, 1, OWN * LON), everyone, split_axis=0, concat_axis=0, tiled=True
    ).reshape(BINS, LON)
    finished = source_update(rank, rows, land_mask, quad_first, quad_second, quad_output)
    return finished.reshape(BINS, 1, LON)


def solution(mesh):
    return jax.shard_map(
        shards,
        mesh=mesh,
        in_specs=(
            P(None, ("space", "spec"), None),
            P(),
            P(),
            P(),
            P(),
            P("space", None),
            P("space"),
            P("space"),
            P("space"),
        ),
        out_specs=P(None, ("space", "spec"), None),
        check_vma=False,
    )
```

```python
import math

import jax
import jax.numpy as jnp
from jax import lax
from jax.experimental import pallas as pl
from jax.experimental.pallas import tpu as pltpu
from jax.sharding import PartitionSpec as P

DIRS = 24
SUBSTEPS = 6
FREQS = 32
BINS = 768
LON = 128
LAT = 256
ROWS = 8
SLOTS = 4096
OWN = 3
SENT = 5
STEPS = 32
PIECES = 2 * OWN + 1
step_weight = 0.25
grid_factors = (1.0, 0.55, 0.3)


def tendency_of(state, first, second, output, wait):
    rounded = state.T.astype(jnp.bfloat16)
    wait(0)
    one = jnp.dot(rounded, first[...], preferred_element_type=jnp.float32)
    wait(1)
    two = jnp.dot(rounded, second[...], preferred_element_type=jnp.float32)
    product = (one * two).astype(jnp.bfloat16)
    wait(2)
    return jnp.dot(product, output[...], preferred_element_type=jnp.float32).T


def slot_row(rank, dest, src, into):
    below = lax.broadcasted_iota(jnp.int32, (LON, LON), 0)
    along = lax.broadcasted_iota(jnp.int32, (LON, LON), 1)
    turned = [jnp.broadcast_to(dest[h : h + 1, :], (LON, LON)).T for h in range(2)]
    total = jnp.zeros((1, LON), jnp.int32)
    for h in range(2):
        same = dest[h : h + 1, :] == turned[h]
        earlier = jnp.sum(jnp.where(same & (below < along), 1, 0), axis=0, keepdims=True)
        if h:
            earlier += jnp.sum(jnp.where(dest[1:2, :] == turned[0], 1, 0), axis=0, keepdims=True)
        to = dest[h : h + 1, :]
        mine = (to % 4 == rank // 2) & (to // 16 == rank % 2)
        cells = src[h : h + 1, :] * (ROWS * LON) + into[h : h + 1, :]
        key = jnp.where(mine, cells * 64 + (to // 4 % 4) * 16 + earlier, -1)
        key = jnp.broadcast_to(key, (LON, LON)).T
        chosen = (key >= 0) & (key % 64 == along % 64)
        value = jnp.where(along < 64, key // (64 * ROWS * LON), key // 64 % (ROWS * LON) + 1)
        total += jnp.sum(jnp.where(chosen, value, 0), axis=0, keepdims=True)
    return jnp.broadcast_to(total.astype(jnp.float32), (8, LON))


def send_kernel(
    rank,
    field_hbm,
    mask_hbm,
    dest_hbm,
    src_hbm,
    into_hbm,
    first_hbm,
    second_hbm,
    output_hbm,
    out,
    field,
    mask,
    dest,
    src,
    into,
    first,
    second,
    output,
    sourced,
    sems,
):
    pairs = [
        (a.at[pl.ds(k * 256, 256), :], b.at[pl.ds(k * 256, 256), :])
        for a, b in ((first_hbm, first), (second_hbm, second), (output_hbm, output))
        for k in range(3)
    ]
    pairs += [
        (field_hbm, field),
        (mask_hbm, mask),
        (dest_hbm, dest),
        (src_hbm, src),
        (into_hbm, into),
    ]
    copies = [pltpu.make_async_copy(a, b, sems.at[n]) for n, (a, b) in enumerate(pairs)]
    small = range(9, 14)
    for n in (*small, *range(9)):
        copies[n].start()
    for n in small:
        copies[n].wait()
    state = field[...]
    sea = mask[pl.ds(rank[0], 1), :].astype(jnp.float32)
    lists = slot_row(rank[0], dest[...], src[...], into[...])
    wide = jnp.broadcast_to(sea, (8, LON))
    for n in range(LAT // 8):
        out[pl.ds(SENT * 8 * n + OWN, 8, stride=SENT), :] = wide
        out[pl.ds(SENT * 8 * n + OWN + 1, 8, stride=SENT), :] = lists
    def wait(n):
        for k in range(3):
            copies[3 * n + k].wait()

    tendency = tendency_of(state, first, second, output, wait)
    sourced[...] = (state + step_weight * tendency) * sea
    for n in range(LAT // 8):
        for q in range(OWN):
            out[pl.ds(SENT * 8 * n + q, 8, stride=SENT), :] = sourced[pl.ds(OWN * 8 * n + q, 8, stride=OWN), :]


def source_and_pack(rank, field, mask, dest, src, into, first, second, output):
    hbm = pl.BlockSpec(memory_space=pltpu.HBM)
    square = pltpu.VMEM((BINS, BINS), jnp.bfloat16)
    pair = pltpu.VMEM((2, LON), jnp.int32)
    return pl.pallas_call(
        send_kernel,
        out_shape=jax.ShapeDtypeStruct((LAT * SENT, LON), jnp.float32),
        in_specs=[pl.BlockSpec(memory_space=pltpu.SMEM)] + [hbm] * 8,
        out_specs=pl.BlockSpec(memory_space=pltpu.VMEM),
        scratch_shapes=[
            pltpu.VMEM((BINS, LON), jnp.float32),
            pltpu.VMEM((ROWS, LON), jnp.int32),
            pair,
            pair,
            pair,
            square,
            square,
            square,
            pltpu.VMEM((BINS, LON), jnp.float32),
            pltpu.SemaphoreType.DMA((14,)),
        ],
        compiler_params=pltpu.CompilerParams(vmem_limit_bytes=62 * 2**20),
    )(rank, field, mask, dest, src, into, first, second, output)


def finish_kernel(rank, field, mask, first, second, output, out):
    state = field[...]
    sea = mask[pl.ds(rank[0], 1), :].astype(jnp.float32)
    out[...] = (state + step_weight * tendency_of(state, first, second, output, lambda n: None)) * sea


def source_update(rank, field, mask, first, second, output):
    vmem = pl.BlockSpec(memory_space=pltpu.VMEM)
    return pl.pallas_call(
        finish_kernel,
        out_shape=jax.ShapeDtypeStruct((BINS, LON), jnp.float32),
        in_specs=[pl.BlockSpec(memory_space=pltpu.SMEM)] + [vmem] * 5,
        out_specs=vmem,
        compiler_params=pltpu.CompilerParams(vmem_limit_bytes=16 * 2**20),
    )(rank, field, mask, first, second, output)


def minmod(lower, upper):
    return jnp.maximum(jnp.minimum(upper, jnp.maximum(lower, 0.0)), jnp.minimum(lower, 0.0))


def transport_kernel(device, owners, field, out, state, sea, coefs, weighted, columns, summed):
    first_bin = device[0] * OWN
    first_dir = first_bin % DIRS
    north_forward = (first_dir < DIRS // 4) | (first_dir >= DIRS - DIRS // 4)
    east_forward = first_dir < DIRS // 2
    upwind = jnp.where(east_forward, 1, LON - 1)
    downwind = LON - upwind

    def place(i):
        return jnp.where(north_forward, i, STEPS - 1 - i)

    def received(i, n):
        return field[pl.ds(SENT * i + n, 8, stride=SENT * STEPS), :]

    sublane = lax.broadcasted_iota(jnp.int32, (8, LON), 0)
    lane = lax.broadcasted_iota(jnp.int32, (8, LON), 1)

    def below(value):
        return jnp.where(sublane > 0, pltpu.roll(value, 1, 0), 0.0)

    def above(value):
        return jnp.where(sublane < 7, pltpu.roll(value, 7, 0), 0.0)

    def before(value):
        return jnp.where(north_forward, below(value), above(value))

    def after(value):
        return jnp.where(north_forward, above(value), below(value))

    for j in range(4):
        scale = jnp.zeros((8, LON), jnp.float32)
        for g in range(8):
            owner = owners[4 * g + jnp.where(north_forward, j, 3 - j)]
            factor = jnp.where(owner == 0, grid_factors[0], jnp.where(owner == 1, grid_factors[1], grid_factors[2]))
            scale = jnp.where(sublane == g, factor, scale)
        for q in range(OWN):
            splat = jnp.zeros((8, LON), jnp.int32) + (first_bin + q)
            direction = ((splat % DIRS).astype(jnp.float32) + 0.5) * (2.0 * math.pi / DIRS)
            speed = 0.2 + 0.7 * ((splat // DIRS).astype(jnp.float32) + 0.5) / FREQS
            north = jnp.abs(speed * jnp.cos(direction)) * scale
            east = jnp.abs(speed * jnp.sin(direction)) * scale
            for kind, value in enumerate(
                (north, 0.5 * north * (1.0 - north), east, 0.5 * east * (1.0 - east))
            ):
                coefs[(kind * OWN + q) * 4 + j] = value
    for i in range(STEPS):
        sea[place(i)] = received(i, OWN)
        for q in range(OWN):
            state[place(i), q] = received(i, q)

    def coef(kind, q, i):
        return coefs[(kind * OWN + q) * 4 + i // 8]

    def flux(kind, q, i, value, slope):
        return coef(kind, q, i) * value + coef(kind + 1, q, i) * slope

    for step in range(SUBSTEPS):
        here, prev, last, flow = [], [], [], []
        for q in range(OWN):
            start = state[0, q]
            end = state[STEPS - 1, q]
            beyond = after(start)
            slope = minmod(end - state[STEPS - 2, q], beyond - end)
            here.append(start)
            prev.append(start - before(end))
            last.append(beyond)
            flow.append(before(flux(0, q, STEPS - 1, end, slope)))
        for i in range(STEPS):
            for q in range(OWN):
                upper = state[i + 1, q] if i + 1 < STEPS else last[q]
                diff = upper - here[q]
                leaving = flux(0, q, i, here[q], minmod(prev[q], diff))
                value = here[q] - leaving + flow[q]
                here[q], prev[q], flow[q] = upper, diff, leaving
                lower = value - pltpu.roll(value, upwind, 1)
                higher = pltpu.roll(value, downwind, 1) - value
                leaving = flux(2, q, i, value, minmod(lower, higher))
                value = value - leaving + pltpu.roll(leaving, upwind, 1)
                state[i, q] = value * sea[i]

    def spread(row, times):
        pair = jnp.broadcast_to(row, (16, LON)).astype(jnp.bfloat16)
        return jnp.broadcast_to(pair[None], (times, 16, LON)).reshape(times * 16, LON)

    low_index = lax.broadcasted_iota(jnp.int32, (32, LON), 0).astype(jnp.float32).astype(jnp.bfloat16)
    high_index = lax.broadcasted_iota(jnp.int32, (256, LON), 0).astype(jnp.float32).astype(jnp.bfloat16)
    zero = jnp.zeros((), jnp.bfloat16)
    one = jnp.ones((), jnp.bfloat16)
    left_half = lane < 64
    for group in range(4):
        for j in range(4):
            even = received(8 * j + 2 * group, OWN + 1)
            odd = received(8 * j + 2 * group + 1, OWN + 1)
            source = jnp.where(left_half, even, pltpu.roll(odd, 64, 1)).astype(jnp.int32)
            target = jnp.where(left_half, pltpu.roll(even, 64, 1), odd).astype(jnp.int32) - 1
            source_row = source // LON
            source_col = source % LON
            target_row = target // LON
            low = jnp.where(target >= 0, (target_row % 4) * 8 + lane // 16, -1).astype(jnp.float32)
            high = ((target_row // 4) * LON + target % LON).astype(jnp.float32)
            pieces = []
            for q in range(OWN):
                taken = jnp.zeros((8, LON), jnp.float32)
                for r in range(ROWS):
                    row = state[place(8 * j + r), q]
                    taken = jnp.where(source_row == r, jnp.take_along_axis(row, source_col, axis=1), taken)
                coarse = taken.astype(jnp.bfloat16).astype(jnp.float32)
                pieces += [coarse, taken - coarse]
            for g in range(8):
                at = (j * 8 + g) * LON
                hit = low_index == spread(low[g : g + 1, :], 2)
                for n, piece in enumerate(pieces):
                    weighted[group, n * 32 : n * 32 + 32, at : at + LON] = jnp.where(
                        hit, spread(piece[g : g + 1, :], 2), zero
                    )
                weighted[group, 2 * OWN * 32 : PIECES * 32, at : at + LON] = jnp.where(hit, one, zero)
                hit = high_index == spread(high[g : g + 1, :], 16)
                columns[group, :, at : at + LON] = jnp.where(hit, one, zero)
        summed[group] = lax.dot_general(
            weighted[group], columns[group], (((1,), (1,)), ((), ())), preferred_element_type=jnp.float32
        )
        for r in range(ROWS):
            i = 8 * group + r
            top = (r % 4) * 8
            left = (r // 4) * LON

            def block(n):
                return summed[group, n * 32 + top : n * 32 + top + 8, left : left + LON]

            share = 1.0 / (1.0 + block(2 * OWN))
            for q in range(OWN):
                merged = (state[place(i), q] + (block(2 * q) + block(2 * q + 1))) * share
                out[pl.ds(OWN * i + q, 8, stride=OWN * STEPS), :] = merged


def transport(device, owners, field):
    vmem = pl.BlockSpec(memory_space=pltpu.VMEM)
    smem = pl.BlockSpec(memory_space=pltpu.SMEM)
    return pl.pallas_call(
        transport_kernel,
        out_shape=jax.ShapeDtypeStruct((BINS, LON), jnp.float32),
        in_specs=[smem, smem, vmem],
        out_specs=vmem,
        scratch_shapes=[
            pltpu.VMEM((STEPS, OWN, 8, LON), jnp.float32),
            pltpu.VMEM((STEPS, 8, LON), jnp.float32),
            pltpu.VMEM((4 * OWN * 4, 8, LON), jnp.float32),
            pltpu.VMEM((4, PIECES * 32, SLOTS), jnp.bfloat16),
            pltpu.VMEM((4, 256, SLOTS), jnp.bfloat16),
            pltpu.VMEM((4, PIECES * 32, 256), jnp.float32),
        ],
        compiler_params=pltpu.CompilerParams(vmem_limit_bytes=32 * 2**20),
    )(device, owners, field)


def shards(
    spectra,
    quad_first,
    quad_second,
    quad_output,
    owner_map,
    land_mask,
    nest_dest,
    nest_src,
    nest_into,
):
    everyone = ("space", "spec")
    spec_rank = lax.axis_index("spec")
    device = lax.axis_index("space") * lax.axis_size("spec") + spec_rank
    rank = spec_rank.reshape(1)
    sent = source_and_pack(
        rank,
        spectra.reshape(BINS, LON),
        land_mask,
        nest_dest.reshape(2, LON),
        nest_src.reshape(2, LON),
        nest_into.reshape(2, LON),
        quad_first,
        quad_second,
        quad_output,
    )
    banded = lax.all_to_all(
        sent.reshape(LAT, 1, SENT * LON), everyone, split_axis=0, concat_axis=0, tiled=True
    ).reshape(LAT * SENT, LON)
    merged = transport(device.reshape(1), owner_map, banded)
    rows = lax.all_to_all(
        merged.reshape(LAT, 1, OWN * LON), everyone, split_axis=0, concat_axis=0, tiled=True
    ).reshape(BINS, LON)
    finished = source_update(rank, rows, land_mask, quad_first, quad_second, quad_output)
    return finished.reshape(BINS, 1, LON)


def solution(mesh):
    return jax.shard_map(
        shards,
        mesh=mesh,
        in_specs=(
            P(None, ("space", "spec"), None),
            P(),
            P(),
            P(),
            P(),
            P("space", None),
            P("space"),
            P("space"),
            P("space"),
        ),
        out_specs=P(None, ("space", "spec"), None),
        check_vma=False,
    )
```

```python
import math

import jax
import jax.numpy as jnp
from jax import lax
from jax.experimental import pallas as pl
from jax.experimental.pallas import tpu as pltpu
from jax.sharding import PartitionSpec as P

DIRS = 24
SUBSTEPS = 6
FREQS = 32
BINS = 768
LON = 128
LAT = 256
ROWS = 8
OWN = 3
SENT = 5
STEPS = 32
PIECES = 2 * OWN + 1
step_weight = 0.25
grid_factors = (1.0, 0.55, 0.3)


def tendency_of(state, first, second, output, wait):
    rounded = state.T.astype(jnp.bfloat16)
    wait(0)
    one = jnp.dot(rounded, first[...], preferred_element_type=jnp.float32)
    wait(1)
    two = jnp.dot(rounded, second[...], preferred_element_type=jnp.float32)
    product = (one * two).astype(jnp.bfloat16)
    wait(2)
    return jnp.dot(product, output[...], preferred_element_type=jnp.float32).T


def slot_row(rank, dest, src, into):
    below = lax.broadcasted_iota(jnp.int32, (LON, LON), 0)
    along = lax.broadcasted_iota(jnp.int32, (LON, LON), 1)
    turned = [jnp.broadcast_to(dest[h : h + 1, :], (LON, LON)).T for h in range(2)]
    total = jnp.zeros((1, LON), jnp.int32)
    for h in range(2):
        same = dest[h : h + 1, :] == turned[h]
        earlier = jnp.sum(jnp.where(same & (below < along), 1, 0), axis=0, keepdims=True)
        if h:
            earlier += jnp.sum(jnp.where(dest[1:2, :] == turned[0], 1, 0), axis=0, keepdims=True)
        to = dest[h : h + 1, :]
        mine = (to % 4 == rank // 2) & (to // 16 == rank % 2)
        cells = src[h : h + 1, :] * (ROWS * LON) + into[h : h + 1, :]
        key = jnp.where(mine, cells * 64 + (to // 4 % 4) * 16 + earlier, -1)
        key = jnp.broadcast_to(key, (LON, LON)).T
        chosen = (key >= 0) & (key % 64 == along % 64)
        value = jnp.where(along < 64, key // (64 * ROWS * LON), key // 64 % (ROWS * LON) + 1)
        total += jnp.sum(jnp.where(chosen, value, 0), axis=0, keepdims=True)
    return jnp.broadcast_to(total.astype(jnp.float32), (8, LON))


def send_kernel(
    device,
    field_hbm,
    mask_hbm,
    dest_hbm,
    src_hbm,
    into_hbm,
    first_hbm,
    second_hbm,
    output_hbm,
    out,
    field,
    mask,
    dest,
    src,
    into,
    first,
    second,
    output,
    sourced,
    sems,
):
    pairs = [
        (a.at[pl.ds(k * 256, 256), :], b.at[pl.ds(k * 256, 256), :])
        for a, b in ((first_hbm, first), (second_hbm, second), (output_hbm, output))
        for k in range(3)
    ]
    pairs += [
        (field_hbm, field),
        (mask_hbm, mask),
        (dest_hbm, dest),
        (src_hbm, src),
        (into_hbm, into),
    ]
    copies = [pltpu.make_async_copy(a, b, sems.at[n]) for n, (a, b) in enumerate(pairs)]
    small = range(9, 14)
    for n in (*small, *range(9)):
        copies[n].start()
    for n in small:
        copies[n].wait()
    state = field[...]
    rank = device[0] % ROWS
    sea = mask[pl.ds(rank, 1), :].astype(jnp.float32)
    lists = slot_row(rank, dest[...], src[...], into[...])
    wide = jnp.broadcast_to(sea, (8, LON))
    for n in range(LAT // 8):
        out[pl.ds(SENT * 8 * n + OWN, 8, stride=SENT), :] = wide
        out[pl.ds(SENT * 8 * n + OWN + 1, 8, stride=SENT), :] = lists
    def wait(n):
        for k in range(3):
            copies[3 * n + k].wait()

    tendency = tendency_of(state, first, second, output, wait)
    sourced[...] = (state + step_weight * tendency) * sea
    for n in range(LAT // 8):
        for q in range(OWN):
            out[pl.ds(SENT * 8 * n + q, 8, stride=SENT), :] = sourced[pl.ds(OWN * 8 * n + q, 8, stride=OWN), :]


def source_and_pack(rank, field, mask, dest, src, into, first, second, output):
    hbm = pl.BlockSpec(memory_space=pltpu.HBM)
    square = pltpu.VMEM((BINS, BINS), jnp.bfloat16)
    pair = pltpu.VMEM((2, LON), jnp.int32)
    return pl.pallas_call(
        send_kernel,
        out_shape=jax.ShapeDtypeStruct((LAT * SENT, LON), jnp.float32),
        in_specs=[pl.BlockSpec(memory_space=pltpu.SMEM)] + [hbm] * 8,
        out_specs=pl.BlockSpec(memory_space=pltpu.VMEM),
        scratch_shapes=[
            pltpu.VMEM((BINS, LON), jnp.float32),
            pltpu.VMEM((ROWS, LON), jnp.int32),
            pair,
            pair,
            pair,
            square,
            square,
            square,
            pltpu.VMEM((BINS, LON), jnp.float32),
            pltpu.SemaphoreType.DMA((14,)),
        ],
        compiler_params=pltpu.CompilerParams(vmem_limit_bytes=62 * 2**20),
    )(rank, field, mask, dest, src, into, first, second, output)


def finish_kernel(device, field, mask, first, second, output, out):
    state = field[...]
    rank = device[0] % ROWS
    sea = mask[pl.ds(rank, 1), :].astype(jnp.float32)
    out[...] = (state + step_weight * tendency_of(state, first, second, output, lambda n: None)) * sea


def source_update(rank, field, mask, first, second, output):
    vmem = pl.BlockSpec(memory_space=pltpu.VMEM)
    return pl.pallas_call(
        finish_kernel,
        out_shape=jax.ShapeDtypeStruct((BINS, LON), jnp.float32),
        in_specs=[pl.BlockSpec(memory_space=pltpu.SMEM)] + [vmem] * 5,
        out_specs=vmem,
        compiler_params=pltpu.CompilerParams(vmem_limit_bytes=16 * 2**20),
    )(rank, field, mask, first, second, output)


def minmod(lower, upper):
    return jnp.maximum(jnp.minimum(upper, jnp.maximum(lower, 0.0)), jnp.minimum(lower, 0.0))


def transport_kernel(device, owners, field, out, state, sea, coefs, summed):
    first_bin = device[0] * OWN
    first_dir = first_bin % DIRS
    north_forward = (first_dir < DIRS // 4) | (first_dir >= DIRS - DIRS // 4)
    east_forward = first_dir < DIRS // 2
    upwind = jnp.where(east_forward, 1, LON - 1)
    downwind = LON - upwind

    def place(i):
        return jnp.where(north_forward, i, STEPS - 1 - i)

    def received(i, n):
        return field[pl.ds(SENT * i + n, 8, stride=SENT * STEPS), :]

    sublane = lax.broadcasted_iota(jnp.int32, (8, LON), 0)
    lane = lax.broadcasted_iota(jnp.int32, (8, LON), 1)

    def below(value):
        return jnp.where(sublane > 0, pltpu.roll(value, 1, 0), 0.0)

    def above(value):
        return jnp.where(sublane < 7, pltpu.roll(value, 7, 0), 0.0)

    def before(value):
        return jnp.where(north_forward, below(value), above(value))

    def after(value):
        return jnp.where(north_forward, above(value), below(value))

    for j in range(4):
        scale = jnp.zeros((8, LON), jnp.float32)
        for g in range(8):
            owner = owners[4 * g + jnp.where(north_forward, j, 3 - j)]
            factor = jnp.where(owner == 0, grid_factors[0], jnp.where(owner == 1, grid_factors[1], grid_factors[2]))
            scale = jnp.where(sublane == g, factor, scale)
        for q in range(OWN):
            splat = jnp.zeros((8, LON), jnp.int32) + (first_bin + q)
            direction = ((splat % DIRS).astype(jnp.float32) + 0.5) * (2.0 * math.pi / DIRS)
            speed = 0.2 + 0.7 * ((splat // DIRS).astype(jnp.float32) + 0.5) / FREQS
            north = jnp.abs(speed * jnp.cos(direction)) * scale
            east = jnp.abs(speed * jnp.sin(direction)) * scale
            for kind, value in enumerate(
                (north, 0.5 * north * (1.0 - north), east, 0.5 * east * (1.0 - east))
            ):
                coefs[(kind * OWN + q) * 4 + j] = value
    for i in range(STEPS):
        sea[place(i)] = received(i, OWN)
        for q in range(OWN):
            state[place(i), q] = received(i, q)

    def coef(kind, q, i):
        return coefs[(kind * OWN + q) * 4 + i // 8]

    def flux(kind, q, i, value, slope):
        return coef(kind, q, i) * value + coef(kind + 1, q, i) * slope

    for step in range(SUBSTEPS):
        here, prev, last, flow = [], [], [], []
        for q in range(OWN):
            start = state[0, q]
            end = state[STEPS - 1, q]
            beyond = after(start)
            slope = minmod(end - state[STEPS - 2, q], beyond - end)
            here.append(start)
            prev.append(start - before(end))
            last.append(beyond)
            flow.append(before(flux(0, q, STEPS - 1, end, slope)))
        for i in range(STEPS):
            for q in range(OWN):
                upper = state[i + 1, q] if i + 1 < STEPS else last[q]
                diff = upper - here[q]
                leaving = flux(0, q, i, here[q], minmod(prev[q], diff))
                value = here[q] - leaving + flow[q]
                here[q], prev[q], flow[q] = upper, diff, leaving
                lower = value - pltpu.roll(value, upwind, 1)
                higher = pltpu.roll(value, downwind, 1) - value
                leaving = flux(2, q, i, value, minmod(lower, higher))
                value = value - leaving + pltpu.roll(leaving, upwind, 1)
                state[i, q] = value * sea[i]

    def spread(row, times):
        pair = jnp.broadcast_to(row, (16, LON)).astype(jnp.bfloat16)
        return jnp.broadcast_to(pair[None], (times, 16, LON)).reshape(times * 16, LON)

    low_index = lax.broadcasted_iota(jnp.int32, (32, LON), 0).astype(jnp.float32).astype(jnp.bfloat16)
    high_index = lax.broadcasted_iota(jnp.int32, (256, LON), 0).astype(jnp.float32).astype(jnp.bfloat16)
    zero = jnp.zeros((), jnp.bfloat16)
    one = jnp.ones((), jnp.bfloat16)
    left_half = lane < 64
    for group in range(4):
        for j in range(4):
            even = received(8 * j + 2 * group, OWN + 1)
            odd = received(8 * j + 2 * group + 1, OWN + 1)
            source = jnp.where(left_half, even, pltpu.roll(odd, 64, 1)).astype(jnp.int32)
            target = jnp.where(left_half, pltpu.roll(even, 64, 1), odd).astype(jnp.int32) - 1
            source_row = source // LON
            source_col = source % LON
            target_row = target // LON
            low = jnp.where(target >= 0, (target_row % 4) * 8 + lane // 16, -1).astype(jnp.float32)
            high = ((target_row // 4) * LON + target % LON).astype(jnp.float32)
            pieces = []
            for q in range(OWN):
                taken = jnp.zeros((8, LON), jnp.float32)
                for r in range(ROWS):
                    row = state[place(8 * j + r), q]
                    taken = jnp.where(source_row == r, jnp.take_along_axis(row, source_col, axis=1), taken)
                coarse = taken.astype(jnp.bfloat16).astype(jnp.float32)
                pieces += [coarse, taken - coarse]
            left_sides, right_sides = [], []
            for g in range(8):
                hit = low_index == spread(low[g : g + 1, :], 2)
                parts = [jnp.where(hit, spread(piece[g : g + 1, :], 2), zero) for piece in pieces]
                parts.append(jnp.where(hit, one, zero))
                left_sides.append(jnp.concatenate(parts, axis=0))
                right_sides.append(jnp.where(high_index == spread(high[g : g + 1, :], 16), one, zero))
            part = lax.dot_general(
                jnp.concatenate(left_sides, axis=1),
                jnp.concatenate(right_sides, axis=1),
                (((1,), (1,)), ((), ())),
                preferred_element_type=jnp.float32,
            )
            total = part if j == 0 else total + part
        summed[group] = total
        for r in range(ROWS):
            i = 8 * group + r
            top = (r % 4) * 8
            left = (r // 4) * LON

            def block(n):
                return summed[group, n * 32 + top : n * 32 + top + 8, left : left + LON]

            share = 1.0 / (1.0 + block(2 * OWN))
            for q in range(OWN):
                merged = (state[place(i), q] + (block(2 * q) + block(2 * q + 1))) * share
                out[pl.ds(OWN * i + q, 8, stride=OWN * STEPS), :] = merged


def transport(device, owners, field):
    vmem = pl.BlockSpec(memory_space=pltpu.VMEM)
    smem = pl.BlockSpec(memory_space=pltpu.SMEM)
    return pl.pallas_call(
        transport_kernel,
        out_shape=jax.ShapeDtypeStruct((BINS, LON), jnp.float32),
        in_specs=[smem, smem, vmem],
        out_specs=vmem,
        scratch_shapes=[
            pltpu.VMEM((STEPS, OWN, 8, LON), jnp.float32),
            pltpu.VMEM((STEPS, 8, LON), jnp.float32),
            pltpu.VMEM((4 * OWN * 4, 8, LON), jnp.float32),
            pltpu.VMEM((4, PIECES * 32, 256), jnp.float32),
        ],
        compiler_params=pltpu.CompilerParams(vmem_limit_bytes=32 * 2**20),
    )(device, owners, field)


def shards(
    spectra,
    quad_first,
    quad_second,
    quad_output,
    owner_map,
    land_mask,
    nest_dest,
    nest_src,
    nest_into,
):
    everyone = ("space", "spec")
    spec_rank = lax.axis_index("spec")
    device = (lax.axis_index("space") * lax.axis_size("spec") + spec_rank).reshape(1)
    sent = source_and_pack(
        device,
        spectra.reshape(BINS, LON),
        land_mask,
        nest_dest.reshape(2, LON),
        nest_src.reshape(2, LON),
        nest_into.reshape(2, LON),
        quad_first,
        quad_second,
        quad_output,
    )
    banded = lax.all_to_all(
        sent.reshape(LAT, 1, SENT * LON), everyone, split_axis=0, concat_axis=0, tiled=True
    ).reshape(LAT * SENT, LON)
    merged = transport(device, owner_map, banded)
    rows = lax.all_to_all(
        merged.reshape(LAT, 1, OWN * LON), everyone, split_axis=0, concat_axis=0, tiled=True
    ).reshape(BINS, LON)
    finished = source_update(device, rows, land_mask, quad_first, quad_second, quad_output)
    return finished.reshape(BINS, 1, LON)


def solution(mesh):
    return jax.shard_map(
        shards,
        mesh=mesh,
        in_specs=(
            P(None, ("space", "spec"), None),
            P(),
            P(),
            P(),
            P(),
            P("space", None),
            P("space"),
            P("space"),
            P("space"),
        ),
        out_specs=P(None, ("space", "spec"), None),
        check_vma=False,
    )
```

```python
import math

import jax
import jax.numpy as jnp
from jax import lax
from jax.experimental import pallas as pl
from jax.experimental.pallas import tpu as pltpu
from jax.sharding import PartitionSpec as P

DIRS = 24
SUBSTEPS = 6
FREQS = 32
BINS = 768
LON = 128
LAT = 256
HALF = BINS // 2
ROWS = 8
OWN = 3
SENT = 5
STEPS = 32
PIECES = 2 * OWN + 1
step_weight = 0.25
grid_factors = (1.0, 0.55, 0.3)


def product_of(state, first, second, wait):
    rounded = state.T.astype(jnp.bfloat16)
    wait(0)
    one = jnp.dot(rounded, first[...], preferred_element_type=jnp.float32)
    wait(1)
    two = jnp.dot(rounded, second[...], preferred_element_type=jnp.float32)
    return (one * two).astype(jnp.bfloat16)


def half_update(half, product, field, output, sea):
    at = pl.ds(half * HALF, HALF)
    tendency = jnp.dot(product, output[:, at], preferred_element_type=jnp.float32).T
    return (field[at, :] + step_weight * tendency) * sea


def slot_row(rank, dest, src, into):
    below = lax.broadcasted_iota(jnp.int32, (LON, LON), 0)
    along = lax.broadcasted_iota(jnp.int32, (LON, LON), 1)
    turned = [jnp.broadcast_to(dest[h : h + 1, :], (LON, LON)).T for h in range(2)]
    total = jnp.zeros((1, LON), jnp.int32)
    for h in range(2):
        same = dest[h : h + 1, :] == turned[h]
        earlier = jnp.sum(jnp.where(same & (below < along), 1, 0), axis=0, keepdims=True)
        if h:
            earlier += jnp.sum(jnp.where(dest[1:2, :] == turned[0], 1, 0), axis=0, keepdims=True)
        to = dest[h : h + 1, :]
        mine = (to % 4 == rank // 2) & (to // 16 == rank % 2)
        cells = src[h : h + 1, :] * (ROWS * LON) + into[h : h + 1, :]
        key = jnp.where(mine, cells * 64 + (to // 4 % 4) * 16 + earlier, -1)
        key = jnp.broadcast_to(key, (LON, LON)).T
        chosen = (key >= 0) & (key % 64 == along % 64)
        value = jnp.where(along < 64, key // (64 * ROWS * LON), key // 64 % (ROWS * LON) + 1)
        total += jnp.sum(jnp.where(chosen, value, 0), axis=0, keepdims=True)
    return jnp.broadcast_to(total.astype(jnp.float32), (8, LON))


def send_kernel(
    device,
    field_hbm,
    mask_hbm,
    dest_hbm,
    src_hbm,
    into_hbm,
    first_hbm,
    second_hbm,
    output_hbm,
    out_hbm,
    out,
    field,
    mask,
    dest,
    src,
    into,
    first,
    second,
    output,
    sourced,
    sems,
):
    pairs = [
        (a.at[pl.ds(k * 256, 256), :], b.at[pl.ds(k * 256, 256), :])
        for a, b in ((first_hbm, first), (second_hbm, second))
        for k in range(3)
    ]
    pairs += [(output_hbm.at[:, pl.ds(h * HALF, HALF)], output.at[:, pl.ds(h * HALF, HALF)]) for h in range(2)]
    pairs += [
        (field_hbm, field),
        (mask_hbm, mask),
        (dest_hbm, dest),
        (src_hbm, src),
        (into_hbm, into),
    ]
    copies = [pltpu.make_async_copy(a, b, sems.at[n]) for n, (a, b) in enumerate(pairs)]
    small = range(8, 13)
    for n in (*small, *range(8)):
        copies[n].start()
    for n in small:
        copies[n].wait()
    state = field[...]
    rank = device[0] % ROWS
    sea = mask[pl.ds(rank, 1), :].astype(jnp.float32)
    lists = slot_row(rank, dest[...], src[...], into[...])
    wide = jnp.broadcast_to(sea, (8, LON))
    for n in range(LAT // 8):
        out[pl.ds(SENT * 8 * n + OWN, 8, stride=SENT), :] = wide
        out[pl.ds(SENT * 8 * n + OWN + 1, 8, stride=SENT), :] = lists

    def wait(n):
        for k in range(3):
            copies[3 * n + k].wait()

    product = product_of(state, first, second, wait)
    sends = []
    for half in range(2):
        copies[6 + half].wait()
        sourced[pl.ds(half * HALF, HALF), :] = half_update(half, product, field, output, sea)
        for n in range(half * LAT // 16, (half + 1) * LAT // 16):
            for q in range(OWN):
                out[pl.ds(SENT * 8 * n + q, 8, stride=SENT), :] = sourced[pl.ds(OWN * 8 * n + q, 8, stride=OWN), :]
        rows = pl.ds(half * LAT * SENT // 2, LAT * SENT // 2)
        sends.append(pltpu.make_async_copy(out.at[rows, :], out_hbm.at[rows, :], sems.at[13 + half]))
        sends[half].start()
    for send in sends:
        send.wait()


def source_and_pack(rank, field, mask, dest, src, into, first, second, output):
    hbm = pl.BlockSpec(memory_space=pltpu.HBM)
    square = pltpu.VMEM((BINS, BINS), jnp.bfloat16)
    pair = pltpu.VMEM((2, LON), jnp.int32)
    return pl.pallas_call(
        send_kernel,
        out_shape=jax.ShapeDtypeStruct((LAT * SENT, LON), jnp.float32),
        in_specs=[pl.BlockSpec(memory_space=pltpu.SMEM)] + [hbm] * 8,
        out_specs=hbm,
        scratch_shapes=[
            pltpu.VMEM((LAT * SENT, LON), jnp.float32),
            pltpu.VMEM((BINS, LON), jnp.float32),
            pltpu.VMEM((ROWS, LON), jnp.int32),
            pair,
            pair,
            pair,
            square,
            square,
            square,
            pltpu.VMEM((BINS, LON), jnp.float32),
            pltpu.SemaphoreType.DMA((15,)),
        ],
        compiler_params=pltpu.CompilerParams(vmem_limit_bytes=63 * 2**20),
    )(rank, field, mask, dest, src, into, first, second, output)


def finish_kernel(device, field, mask, first, second, output, out_hbm, out, sems):
    sea = mask[pl.ds(device[0] % ROWS, 1), :].astype(jnp.float32)
    product = product_of(field[...], first, second, lambda n: None)
    sends = []
    for half in range(2):
        at = pl.ds(half * HALF, HALF)
        out[at, :] = half_update(half, product, field, output, sea)
        sends.append(pltpu.make_async_copy(out.at[at, :], out_hbm.at[at, :], sems.at[half]))
        sends[half].start()
    for send in sends:
        send.wait()


def source_update(device, field, mask, first, second, output):
    vmem = pl.BlockSpec(memory_space=pltpu.VMEM)
    return pl.pallas_call(
        finish_kernel,
        out_shape=jax.ShapeDtypeStruct((BINS, LON), jnp.float32),
        in_specs=[pl.BlockSpec(memory_space=pltpu.SMEM)] + [vmem] * 5,
        out_specs=pl.BlockSpec(memory_space=pltpu.HBM),
        scratch_shapes=[pltpu.VMEM((BINS, LON), jnp.float32), pltpu.SemaphoreType.DMA((2,))],
        compiler_params=pltpu.CompilerParams(vmem_limit_bytes=16 * 2**20),
    )(device, field, mask, first, second, output)


def minmod(lower, upper):
    return jnp.maximum(jnp.minimum(upper, jnp.maximum(lower, 0.0)), jnp.minimum(lower, 0.0))


def transport_kernel(device, owners, field, output_hbm, out, output, state, sea, coefs, summed, sem):
    fetch = pltpu.make_async_copy(output_hbm, output, sem)
    fetch.start()
    first_bin = device[0] * OWN
    first_dir = first_bin % DIRS
    north_forward = (first_dir < DIRS // 4) | (first_dir >= DIRS - DIRS // 4)
    east_forward = first_dir < DIRS // 2
    upwind = jnp.where(east_forward, 1, LON - 1)
    downwind = LON - upwind

    def place(i):
        return jnp.where(north_forward, i, STEPS - 1 - i)

    def received(i, n):
        return field[pl.ds(SENT * i + n, 8, stride=SENT * STEPS), :]

    sublane = lax.broadcasted_iota(jnp.int32, (8, LON), 0)
    lane = lax.broadcasted_iota(jnp.int32, (8, LON), 1)

    def below(value):
        return jnp.where(sublane > 0, pltpu.roll(value, 1, 0), 0.0)

    def above(value):
        return jnp.where(sublane < 7, pltpu.roll(value, 7, 0), 0.0)

    def before(value):
        return jnp.where(north_forward, below(value), above(value))

    def after(value):
        return jnp.where(north_forward, above(value), below(value))

    for j in range(4):
        scale = jnp.zeros((8, LON), jnp.float32)
        for g in range(8):
            owner = owners[4 * g + jnp.where(north_forward, j, 3 - j)]
            factor = jnp.where(owner == 0, grid_factors[0], jnp.where(owner == 1, grid_factors[1], grid_factors[2]))
            scale = jnp.where(sublane == g, factor, scale)
        for q in range(OWN):
            splat = jnp.zeros((8, LON), jnp.int32) + (first_bin + q)
            direction = ((splat % DIRS).astype(jnp.float32) + 0.5) * (2.0 * math.pi / DIRS)
            speed = 0.2 + 0.7 * ((splat // DIRS).astype(jnp.float32) + 0.5) / FREQS
            north = jnp.abs(speed * jnp.cos(direction)) * scale
            east = jnp.abs(speed * jnp.sin(direction)) * scale
            for kind, value in enumerate(
                (north, 0.5 * north * (1.0 - north), east, 0.5 * east * (1.0 - east))
            ):
                coefs[(kind * OWN + q) * 4 + j] = value
    for i in range(STEPS):
        sea[place(i)] = received(i, OWN)
        for q in range(OWN):
            state[place(i), q] = received(i, q)

    def coef(kind, q, i):
        return coefs[(kind * OWN + q) * 4 + i // 8]

    def flux(kind, q, i, value, slope):
        return coef(kind, q, i) * value + coef(kind + 1, q, i) * slope

    for step in range(SUBSTEPS):
        here, prev, last, flow = [], [], [], []
        for q in range(OWN):
            start = state[0, q]
            end = state[STEPS - 1, q]
            beyond = after(start)
            slope = minmod(end - state[STEPS - 2, q], beyond - end)
            here.append(start)
            prev.append(start - before(end))
            last.append(beyond)
            flow.append(before(flux(0, q, STEPS - 1, end, slope)))
        for i in range(STEPS):
            for q in range(OWN):
                upper = state[i + 1, q] if i + 1 < STEPS else last[q]
                diff = upper - here[q]
                leaving = flux(0, q, i, here[q], minmod(prev[q], diff))
                value = here[q] - leaving + flow[q]
                here[q], prev[q], flow[q] = upper, diff, leaving
                lower = value - pltpu.roll(value, upwind, 1)
                higher = pltpu.roll(value, downwind, 1) - value
                leaving = flux(2, q, i, value, minmod(lower, higher))
                value = value - leaving + pltpu.roll(leaving, upwind, 1)
                state[i, q] = value * sea[i]

    def spread(row, times):
        pair = jnp.broadcast_to(row, (16, LON)).astype(jnp.bfloat16)
        return jnp.broadcast_to(pair[None], (times, 16, LON)).reshape(times * 16, LON)

    low_index = lax.broadcasted_iota(jnp.int32, (32, LON), 0).astype(jnp.float32).astype(jnp.bfloat16)
    high_index = lax.broadcasted_iota(jnp.int32, (256, LON), 0).astype(jnp.float32).astype(jnp.bfloat16)
    zero = jnp.zeros((), jnp.bfloat16)
    one = jnp.ones((), jnp.bfloat16)
    left_half = lane < 64
    for group in range(4):
        for j in range(4):
            even = received(8 * j + 2 * group, OWN + 1)
            odd = received(8 * j + 2 * group + 1, OWN + 1)
            source = jnp.where(left_half, even, pltpu.roll(odd, 64, 1)).astype(jnp.int32)
            target = jnp.where(left_half, pltpu.roll(even, 64, 1), odd).astype(jnp.int32) - 1
            source_row = source // LON
            source_col = source % LON
            target_row = target // LON
            low = jnp.where(target >= 0, (target_row % 4) * 8 + lane // 16, -1).astype(jnp.float32)
            high = ((target_row // 4) * LON + target % LON).astype(jnp.float32)
            pieces = []
            for q in range(OWN):
                taken = jnp.zeros((8, LON), jnp.float32)
                for r in range(ROWS):
                    row = state[place(8 * j + r), q]
                    taken = jnp.where(source_row == r, jnp.take_along_axis(row, source_col, axis=1), taken)
                coarse = taken.astype(jnp.bfloat16).astype(jnp.float32)
                pieces += [coarse, taken - coarse]
            left_sides, right_sides = [], []
            for g in range(8):
                hit = low_index == spread(low[g : g + 1, :], 2)
                parts = [jnp.where(hit, spread(piece[g : g + 1, :], 2), zero) for piece in pieces]
                parts.append(jnp.where(hit, one, zero))
                left_sides.append(jnp.concatenate(parts, axis=0))
                right_sides.append(jnp.where(high_index == spread(high[g : g + 1, :], 16), one, zero))
            part = lax.dot_general(
                jnp.concatenate(left_sides, axis=1),
                jnp.concatenate(right_sides, axis=1),
                (((1,), (1,)), ((), ())),
                preferred_element_type=jnp.float32,
            )
            total = part if j == 0 else total + part
        summed[group] = total
        for r in range(ROWS):
            i = 8 * group + r
            top = (r % 4) * 8
            left = (r // 4) * LON

            def block(n):
                return summed[group, n * 32 + top : n * 32 + top + 8, left : left + LON]

            share = 1.0 / (1.0 + block(2 * OWN))
            for q in range(OWN):
                merged = (state[place(i), q] + (block(2 * q) + block(2 * q + 1))) * share
                out[pl.ds(OWN * i + q, 8, stride=OWN * STEPS), :] = merged
    fetch.wait()


def transport(device, owners, field, output):
    vmem = pl.BlockSpec(memory_space=pltpu.VMEM)
    smem = pl.BlockSpec(memory_space=pltpu.SMEM)
    return pl.pallas_call(
        transport_kernel,
        out_shape=[jax.ShapeDtypeStruct((BINS, LON), jnp.float32), jax.ShapeDtypeStruct((BINS, BINS), jnp.bfloat16)],
        in_specs=[smem, smem, vmem, pl.BlockSpec(memory_space=pltpu.HBM)],
        out_specs=[vmem, vmem],
        scratch_shapes=[
            pltpu.VMEM((STEPS, OWN, 8, LON), jnp.float32),
            pltpu.VMEM((STEPS, 8, LON), jnp.float32),
            pltpu.VMEM((4 * OWN * 4, 8, LON), jnp.float32),
            pltpu.VMEM((4, PIECES * 32, 256), jnp.float32),
            pltpu.SemaphoreType.DMA,
        ],
        compiler_params=pltpu.CompilerParams(vmem_limit_bytes=32 * 2**20),
    )(device, owners, field, output)


def shards(
    spectra,
    quad_first,
    quad_second,
    quad_output,
    owner_map,
    land_mask,
    nest_dest,
    nest_src,
    nest_into,
):
    everyone = ("space", "spec")
    spec_rank = lax.axis_index("spec")
    device = (lax.axis_index("space") * lax.axis_size("spec") + spec_rank).reshape(1)
    sent = source_and_pack(
        device,
        spectra.reshape(BINS, LON),
        land_mask,
        nest_dest.reshape(2, LON),
        nest_src.reshape(2, LON),
        nest_into.reshape(2, LON),
        quad_first,
        quad_second,
        quad_output,
    )
    banded = lax.all_to_all(
        sent.reshape(LAT, 1, SENT * LON), everyone, split_axis=0, concat_axis=0, tiled=True
    ).reshape(LAT * SENT, LON)
    merged, output = transport(device, owner_map, banded, quad_output)
    rows = lax.all_to_all(
        merged.reshape(LAT, 1, OWN * LON), everyone, split_axis=0, concat_axis=0, tiled=True
    ).reshape(BINS, LON)
    finished = source_update(device, rows, land_mask, quad_first, quad_second, output)
    return finished.reshape(BINS, 1, LON)


def solution(mesh):
    return jax.shard_map(
        shards,
        mesh=mesh,
        in_specs=(
            P(None, ("space", "spec"), None),
            P(),
            P(),
            P(),
            P(),
            P("space", None),
            P("space"),
            P("space"),
            P("space"),
        ),
        out_specs=P(None, ("space", "spec"), None),
        check_vma=False,
    )
```

```python
import math

import jax
import jax.numpy as jnp
from jax import lax
from jax.experimental import pallas as pl
from jax.experimental.pallas import tpu as pltpu
from jax.sharding import PartitionSpec as P

DIRS = 24
SUBSTEPS = 6
FREQS = 32
BINS = 768
LON = 128
LAT = 256
ROWS = 8
OWN = 3
SENT = 5
STEPS = 32
PIECES = OWN + 1
step_weight = 0.25
grid_factors = (1.0, 0.55, 0.3)


def tendency_of(state, first, second, output, wait):
    rounded = state.T.astype(jnp.bfloat16)
    wait(0)
    one = jnp.dot(rounded, first[...], preferred_element_type=jnp.float32)
    wait(1)
    two = jnp.dot(rounded, second[...], preferred_element_type=jnp.float32)
    product = (one * two).astype(jnp.bfloat16)
    wait(2)
    return jnp.dot(product, output[...], preferred_element_type=jnp.float32).T


def slot_row(rank, dest, src, into):
    below = lax.broadcasted_iota(jnp.int32, (LON, LON), 0)
    along = lax.broadcasted_iota(jnp.int32, (LON, LON), 1)
    turned = [jnp.broadcast_to(dest[h : h + 1, :], (LON, LON)).T for h in range(2)]
    total = jnp.zeros((1, LON), jnp.int32)
    for h in range(2):
        same = dest[h : h + 1, :] == turned[h]
        earlier = jnp.sum(jnp.where(same & (below < along), 1, 0), axis=0, keepdims=True)
        if h:
            earlier += jnp.sum(jnp.where(dest[1:2, :] == turned[0], 1, 0), axis=0, keepdims=True)
        to = dest[h : h + 1, :]
        mine = (to % 4 == rank // 2) & (to // 16 == rank % 2)
        cells = src[h : h + 1, :] * (ROWS * LON) + into[h : h + 1, :]
        key = jnp.where(mine, cells * 64 + (to // 4 % 4) * 16 + earlier, -1)
        key = jnp.broadcast_to(key, (LON, LON)).T
        chosen = (key >= 0) & (key % 64 == along % 64)
        value = jnp.where(along < 64, key // (64 * ROWS * LON), key // 64 % (ROWS * LON) + 1)
        total += jnp.sum(jnp.where(chosen, value, 0), axis=0, keepdims=True)
    return jnp.broadcast_to(total.astype(jnp.float32), (8, LON))


def send_kernel(
    device,
    field_hbm,
    mask_hbm,
    dest_hbm,
    src_hbm,
    into_hbm,
    first_hbm,
    second_hbm,
    output_hbm,
    out,
    field,
    mask,
    dest,
    src,
    into,
    first,
    second,
    output,
    sourced,
    sems,
):
    pairs = [
        (a.at[pl.ds(k * 256, 256), :], b.at[pl.ds(k * 256, 256), :])
        for a, b in ((first_hbm, first), (second_hbm, second), (output_hbm, output))
        for k in range(3)
    ]
    pairs += [
        (field_hbm, field),
        (mask_hbm, mask),
        (dest_hbm, dest),
        (src_hbm, src),
        (into_hbm, into),
    ]
    copies = [pltpu.make_async_copy(a, b, sems.at[n]) for n, (a, b) in enumerate(pairs)]
    small = range(9, 14)
    for n in (*small, *range(9)):
        copies[n].start()
    for n in small:
        copies[n].wait()
    state = field[...]
    rank = device[0] % ROWS
    sea = mask[pl.ds(rank, 1), :].astype(jnp.float32)
    lists = slot_row(rank, dest[...], src[...], into[...])
    wide = jnp.broadcast_to(sea, (8, LON))
    for n in range(LAT // 8):
        out[pl.ds(SENT * 8 * n + OWN, 8, stride=SENT), :] = wide
        out[pl.ds(SENT * 8 * n + OWN + 1, 8, stride=SENT), :] = lists
    def wait(n):
        for k in range(3):
            copies[3 * n + k].wait()

    tendency = tendency_of(state, first, second, output, wait)
    sourced[...] = (state + step_weight * tendency) * sea
    for n in range(LAT // 8):
        for q in range(OWN):
            out[pl.ds(SENT * 8 * n + q, 8, stride=SENT), :] = sourced[pl.ds(OWN * 8 * n + q, 8, stride=OWN), :]


def source_and_pack(rank, field, mask, dest, src, into, first, second, output):
    hbm = pl.BlockSpec(memory_space=pltpu.HBM)
    square = pltpu.VMEM((BINS, BINS), jnp.bfloat16)
    pair = pltpu.VMEM((2, LON), jnp.int32)
    return pl.pallas_call(
        send_kernel,
        out_shape=jax.ShapeDtypeStruct((LAT * SENT, LON), jnp.float32),
        in_specs=[pl.BlockSpec(memory_space=pltpu.SMEM)] + [hbm] * 8,
        out_specs=pl.BlockSpec(memory_space=pltpu.VMEM),
        scratch_shapes=[
            pltpu.VMEM((BINS, LON), jnp.float32),
            pltpu.VMEM((ROWS, LON), jnp.int32),
            pair,
            pair,
            pair,
            square,
            square,
            square,
            pltpu.VMEM((BINS, LON), jnp.float32),
            pltpu.SemaphoreType.DMA((14,)),
        ],
        compiler_params=pltpu.CompilerParams(vmem_limit_bytes=62 * 2**20),
    )(rank, field, mask, dest, src, into, first, second, output)


def finish_kernel(device, field, mask, first, second, output, out):
    state = field[...]
    rank = device[0] % ROWS
    sea = mask[pl.ds(rank, 1), :].astype(jnp.float32)
    out[...] = (state + step_weight * tendency_of(state, first, second, output, lambda n: None)) * sea


def source_update(rank, field, mask, first, second, output):
    vmem = pl.BlockSpec(memory_space=pltpu.VMEM)
    return pl.pallas_call(
        finish_kernel,
        out_shape=jax.ShapeDtypeStruct((BINS, LON), jnp.float32),
        in_specs=[pl.BlockSpec(memory_space=pltpu.SMEM)] + [vmem] * 5,
        out_specs=vmem,
        compiler_params=pltpu.CompilerParams(vmem_limit_bytes=16 * 2**20),
    )(rank, field, mask, first, second, output)


def minmod(lower, upper):
    return jnp.maximum(jnp.minimum(upper, jnp.maximum(lower, 0.0)), jnp.minimum(lower, 0.0))


def transport_kernel(device, owners, field, out, state, sea, coefs, summed):
    first_bin = device[0] * OWN
    first_dir = first_bin % DIRS
    north_forward = (first_dir < DIRS // 4) | (first_dir >= DIRS - DIRS // 4)
    east_forward = first_dir < DIRS // 2
    upwind = jnp.where(east_forward, 1, LON - 1)
    downwind = LON - upwind

    def place(i):
        return jnp.where(north_forward, i, STEPS - 1 - i)

    def received(i, n):
        return field[pl.ds(SENT * i + n, 8, stride=SENT * STEPS), :]

    sublane = lax.broadcasted_iota(jnp.int32, (8, LON), 0)
    lane = lax.broadcasted_iota(jnp.int32, (8, LON), 1)

    def below(value):
        return jnp.where(sublane > 0, pltpu.roll(value, 1, 0), 0.0)

    def above(value):
        return jnp.where(sublane < 7, pltpu.roll(value, 7, 0), 0.0)

    def before(value):
        return jnp.where(north_forward, below(value), above(value))

    def after(value):
        return jnp.where(north_forward, above(value), below(value))

    for j in range(4):
        scale = jnp.zeros((8, LON), jnp.float32)
        for g in range(8):
            owner = owners[4 * g + jnp.where(north_forward, j, 3 - j)]
            factor = jnp.where(owner == 0, grid_factors[0], jnp.where(owner == 1, grid_factors[1], grid_factors[2]))
            scale = jnp.where(sublane == g, factor, scale)
        for q in range(OWN):
            splat = jnp.zeros((8, LON), jnp.int32) + (first_bin + q)
            direction = ((splat % DIRS).astype(jnp.float32) + 0.5) * (2.0 * math.pi / DIRS)
            speed = 0.2 + 0.7 * ((splat // DIRS).astype(jnp.float32) + 0.5) / FREQS
            north = jnp.abs(speed * jnp.cos(direction)) * scale
            east = jnp.abs(speed * jnp.sin(direction)) * scale
            for kind, value in enumerate(
                (north, 0.5 * north * (1.0 - north), east, 0.5 * east * (1.0 - east))
            ):
                coefs[(kind * OWN + q) * 4 + j] = value
    for i in range(STEPS):
        sea[place(i)] = received(i, OWN)
        for q in range(OWN):
            state[place(i), q] = received(i, q)

    def coef(kind, q, i):
        return coefs[(kind * OWN + q) * 4 + i // 8]

    def flux(kind, q, i, value, slope):
        return coef(kind, q, i) * value + coef(kind + 1, q, i) * slope

    for step in range(SUBSTEPS):
        here, prev, last, flow = [], [], [], []
        for q in range(OWN):
            start = state[0, q]
            end = state[STEPS - 1, q]
            beyond = after(start)
            slope = minmod(end - state[STEPS - 2, q], beyond - end)
            here.append(start)
            prev.append(start - before(end))
            last.append(beyond)
            flow.append(before(flux(0, q, STEPS - 1, end, slope)))
        for i in range(STEPS):
            for q in range(OWN):
                upper = state[i + 1, q] if i + 1 < STEPS else last[q]
                diff = upper - here[q]
                leaving = flux(0, q, i, here[q], minmod(prev[q], diff))
                value = here[q] - leaving + flow[q]
                here[q], prev[q], flow[q] = upper, diff, leaving
                lower = value - pltpu.roll(value, upwind, 1)
                higher = pltpu.roll(value, downwind, 1) - value
                leaving = flux(2, q, i, value, minmod(lower, higher))
                value = value - leaving + pltpu.roll(leaving, upwind, 1)
                state[i, q] = value * sea[i]

    def spread(row, times):
        pair = jnp.broadcast_to(row, (16, LON)).astype(jnp.bfloat16)
        return jnp.broadcast_to(pair[None], (times, 16, LON)).reshape(times * 16, LON)

    low_index = lax.broadcasted_iota(jnp.int32, (32, LON), 0).astype(jnp.float32).astype(jnp.bfloat16)
    high_index = lax.broadcasted_iota(jnp.int32, (256, LON), 0).astype(jnp.float32).astype(jnp.bfloat16)
    zero = jnp.zeros((), jnp.bfloat16)
    one = jnp.ones((), jnp.bfloat16)
    left_half = lane < 64
    for group in range(4):
        for j in range(4):
            even = received(8 * j + 2 * group, OWN + 1)
            odd = received(8 * j + 2 * group + 1, OWN + 1)
            source = jnp.where(left_half, even, pltpu.roll(odd, 64, 1)).astype(jnp.int32)
            target = jnp.where(left_half, pltpu.roll(even, 64, 1), odd).astype(jnp.int32) - 1
            source_row = source // LON
            source_col = source % LON
            target_row = target // LON
            low = jnp.where(target >= 0, (target_row % 4) * 8 + lane // 16, -1).astype(jnp.float32)
            high = ((target_row // 4) * LON + target % LON).astype(jnp.float32)
            pieces = []
            for q in range(OWN):
                taken = jnp.zeros((8, LON), jnp.float32)
                for r in range(ROWS):
                    row = state[place(8 * j + r), q]
                    taken = jnp.where(source_row == r, jnp.take_along_axis(row, source_col, axis=1), taken)
                pieces.append(taken)
            left_sides, right_sides = [], []
            for g in range(8):
                hit = low_index == spread(low[g : g + 1, :], 2)
                parts = [jnp.where(hit, spread(piece[g : g + 1, :], 2), zero) for piece in pieces]
                parts.append(jnp.where(hit, one, zero))
                left_sides.append(jnp.concatenate(parts, axis=0))
                right_sides.append(jnp.where(high_index == spread(high[g : g + 1, :], 16), one, zero))
            part = lax.dot_general(
                jnp.concatenate(left_sides, axis=1),
                jnp.concatenate(right_sides, axis=1),
                (((1,), (1,)), ((), ())),
                preferred_element_type=jnp.float32,
            )
            total = part if j == 0 else total + part
        summed[group] = total
        for r in range(ROWS):
            i = 8 * group + r
            top = (r % 4) * 8
            left = (r // 4) * LON

            def block(n):
                return summed[group, n * 32 + top : n * 32 + top + 8, left : left + LON]

            share = 1.0 / (1.0 + block(OWN))
            for q in range(OWN):
                merged = (state[place(i), q] + block(q)) * share
                out[pl.ds(OWN * i + q, 8, stride=OWN * STEPS), :] = merged


def transport(device, owners, field):
    vmem = pl.BlockSpec(memory_space=pltpu.VMEM)
    smem = pl.BlockSpec(memory_space=pltpu.SMEM)
    return pl.pallas_call(
        transport_kernel,
        out_shape=jax.ShapeDtypeStruct((BINS, LON), jnp.float32),
        in_specs=[smem, smem, vmem],
        out_specs=vmem,
        scratch_shapes=[
            pltpu.VMEM((STEPS, OWN, 8, LON), jnp.float32),
            pltpu.VMEM((STEPS, 8, LON), jnp.float32),
            pltpu.VMEM((4 * OWN * 4, 8, LON), jnp.float32),
            pltpu.VMEM((4, PIECES * 32, 256), jnp.float32),
        ],
        compiler_params=pltpu.CompilerParams(vmem_limit_bytes=32 * 2**20),
    )(device, owners, field)


def shards(
    spectra,
    quad_first,
    quad_second,
    quad_output,
    owner_map,
    land_mask,
    nest_dest,
    nest_src,
    nest_into,
):
    everyone = ("space", "spec")
    spec_rank = lax.axis_index("spec")
    device = (lax.axis_index("space") * lax.axis_size("spec") + spec_rank).reshape(1)
    sent = source_and_pack(
        device,
        spectra.reshape(BINS, LON),
        land_mask,
        nest_dest.reshape(2, LON),
        nest_src.reshape(2, LON),
        nest_into.reshape(2, LON),
        quad_first,
        quad_second,
        quad_output,
    )
    banded = lax.all_to_all(
        sent.reshape(LAT, 1, SENT * LON), everyone, split_axis=0, concat_axis=0, tiled=True
    ).reshape(LAT * SENT, LON)
    merged = transport(device, owner_map, banded)
    rows = lax.all_to_all(
        merged.reshape(LAT, 1, OWN * LON), everyone, split_axis=0, concat_axis=0, tiled=True
    ).reshape(BINS, LON)
    finished = source_update(device, rows, land_mask, quad_first, quad_second, quad_output)
    return finished.reshape(BINS, 1, LON)


def solution(mesh):
    return jax.shard_map(
        shards,
        mesh=mesh,
        in_specs=(
            P(None, ("space", "spec"), None),
            P(),
            P(),
            P(),
            P(),
            P("space", None),
            P("space"),
            P("space"),
            P("space"),
        ),
        out_specs=P(None, ("space", "spec"), None),
        check_vma=False,
    )
```
